768 devices in a mesh: section: 192 (over y, z_lo, x, core), expert: 4 (over z_hi).
Axes of the slice: x: 4, y: 8, z: 12 (z_hi: 4, z_lo: 3; z = z_hi * 3 + z_lo), core: 2. Of those that a mesh axis runs over, the one named last changes fastest.
Arguments:
- routes: int32 [192, 2, 256, 2], P('section'), may hold values from 0 to 3, all different within a row; in each aligned block of 256 rows (0 to 255, 256 to 511, ..., all dimensions but the last counted through in order) at most 192 rows name the same one
- x_blocks: bfloat16 [192, 2, 4, 192, 1024], P('section', None, 'expert'), may hold values from -6 to 6
- d_hidden: bfloat16 [192, 2, 4, 192, 384], P('section', None, 'expert'), may hold values from -3 to 3
- weights: bfloat16 [192, 4, 1024, 768], P('section', 'expert'), as said below
Outputs:
- d_in: bfloat16 [192, 256, 2, 1024], P('section', 'expert')
- d_weights: bfloat16 [192, 4, 1024, 768], P('section', 'expert')
The draws below stay inside these ranges and needn't reach their ends.
Inputs may be any that keep to these rules, and one draw needn't show every extreme that they name: weights[s] equals weights[(s + 96) mod 192] for every section s: twin sections hold copies of one layer. `routes`: each token names 2 different experts; in each section and direction no expert is named by more than 192 tokens, and in every draw some expert is named by exactly 192 tokens of some section and direction.
All inputs are finite; a program needn't handle non-finite values.
Results may differ from the reference program's by a relative error of at most 0.0059.
Values may be sent and summed in bfloat16 or wider, within the bound.
A program may use at most 32 MiB of HBM per device.

```python
import math
import jax
import jax.numpy as jnp
import numpy as np
from jax import lax

D = 1024
FF = 384
TOP = 2
TOKS = 256
CAP = 192
EXPERTS = 4
SECTIONS = 192


def draw_weights(key, part):
    half_count = SECTIONS // 2
    shape = (half_count, EXPERTS, D, 2 * FF)
    base = jax.random.normal(key, shape, jnp.float32)
    base = base * D ** (-0.5)
    return jnp.concatenate([base, base], axis=0).astype(jnp.bfloat16)


def shard_levels(key, shape, cuts, least, top_value):
    def one(axis_at, shards_of):
        draws = jax.random.uniform(jax.random.fold_in(jax.random.fold_in(key, 6), axis_at), (shards_of,), jnp.float32, least / len(cuts), top_value / len(cuts))
        return jnp.repeat(jnp.exp(draws), shape[axis_at] // shards_of).reshape((-1,) + (1,) * (len(shape) - axis_at - 1))

    level = one(*cuts[0])
    for cut in cuts[1:]:
        level = level * one(*cut)
    return level


def assign_block(own_key, own, number, rows, count, top, reach, skew):
    sequence = jax.random.permutation(own_key, count)
    packed, usual = portions_of(count, rows * top, reach, skew, True), portions_of(count, rows * top, reach, skew, False)
    places = jnp.arange(count)

    def named(lengths, turn):
        used = int((lengths > 0).sum())
        fixed = max(1, used // 4)
        passed = fixed + (places - fixed + turn * (used - fixed)) % max(1, count - fixed)
        return jnp.zeros((count,), jnp.int32).at[sequence[jnp.where(places < fixed, places, passed)]].set(jnp.asarray(lengths, jnp.int32))

    lengths = jnp.where(number % 4 == 0, named(packed, number // 4), named(usual, number - number // 4 - 1))
    mixed = jax.random.permutation(jax.random.fold_in(own, 3), count)
    giver, receiver = mixed[0:count // 2 * 2:2], mixed[1:count // 2 * 2:2]
    room = jnp.minimum(lengths[giver] - 1, reach - lengths[receiver]) // 2
    room = jnp.where((giver == sequence[0]) | (receiver == sequence[0]) | (lengths[receiver] == 0), 0, jnp.maximum(room, 0))
    passed = jax.random.randint(jax.random.fold_in(own, 4), (count // 2,), 0, 1 << 20) % (room + 1)
    lengths = lengths.at[giver].add(-passed).at[receiver].add(passed)
    items = jnp.searchsorted(jnp.cumsum(lengths), jnp.arange(rows * top), side="right").astype(jnp.int32)
    listing = items.reshape(top, rows).T
    listing = listing[jax.random.permutation(jax.random.fold_in(own, 1), rows)]
    turn = jax.random.randint(jax.random.fold_in(own, 2), (rows, 1), 0, top)
    return jnp.take_along_axis(listing, (jnp.arange(top)[None, :] + turn) % top, axis=1)


def portions_of(count, total, most, slope, full):
    loads = [(1 << 20) // math.isqrt(standing ** slope) + 1 for standing in range(1, count + 1)]
    largest = most if full else min(most, max(-(-total // count), total * loads[0] // sum(loads)))
    least = 1 if total - largest >= count - 1 else 0
    counts, surplus = [largest] + [least] * (count - 1), total - largest - least * (count - 1)
    while surplus > 0:
        candidates = [i for i in range(1, count) if counts[i] < largest] or [i for i in range(1, count) if counts[i] < most]
        whole, left = sum([loads[i] for i in candidates]), surplus
        for i in candidates:
            addition = min(most - counts[i], max(1, left * loads[i] // whole), surplus)
            counts[i] = counts[i] + addition
            surplus = surplus - addition
    return np.array(counts)


def normal_values(stream_key, shape, deviation, limit, cuts=(), kind=jnp.bfloat16):
    factor_of = shard_levels(stream_key, shape, cuts, -0.22, 0.18) if cuts else 1.0
    result = jax.random.normal(stream_key, shape, jnp.float32) * deviation * factor_of
    return jnp.minimum(jnp.maximum(result, -limit), limit).astype(kind)


def setup_inputs(seed: int = 0) -> dict:
    arg_keys = jax.random.split(jax.random.key(seed), 5)
    routes_keys = jax.random.split(jax.random.fold_in(arg_keys[0], 1), SECTIONS * 2 * TOKS // TOKS)
    routes_turns = jax.random.permutation(jax.random.fold_in(arg_keys[0], 3), SECTIONS * 2 * TOKS // TOKS)
    routes = jax.vmap(lambda own, number: assign_block(jax.random.fold_in(arg_keys[0], 2), own, number, TOKS, EXPERTS, TOP, CAP, 1))(routes_keys, routes_turns).reshape((SECTIONS, 2, TOKS, TOP))
    x_blocks = normal_values(arg_keys[1], (SECTIONS, 2, EXPERTS, CAP, D), 1.0, 6.0, ((0, 192), (2, 4)))
    d_hidden = normal_values(arg_keys[2], (SECTIONS, 2, EXPERTS, CAP, FF), 0.5, 3.0, ((0, 192), (2, 4)))
    weights = draw_weights(jax.random.fold_in(arg_keys[4], 71), 0)
    return dict(routes=routes, x_blocks=x_blocks, d_hidden=d_hidden, weights=weights)


def expert_backward(flat_in, flat_grad, matrix):
    hidden_width = flat_grad.shape[1]
    projected = jnp.dot(flat_in, matrix, preferred_element_type=jnp.float32)
    gate_pre = projected[:, :hidden_width]
    up_pre = projected[:, hidden_width:]
    sigmoid = jax.nn.sigmoid(gate_pre)
    grad_float = flat_grad.astype(jnp.float32)
    grad_gate = grad_float * up_pre * sigmoid * (1.0 + gate_pre * (1.0 - sigmoid))
    grad_up = grad_float * gate_pre * sigmoid
    return jnp.concatenate([grad_gate, grad_up], axis=1).astype(jnp.bfloat16)


def reference(routes, x_blocks, d_hidden, weights):
    capacity = x_blocks.shape[3]
    width = x_blocks.shape[4]
    hidden_width = d_hidden.shape[4]

    def one_section(section_index):
        routing = routes[section_index]

        def one_expert(expert_index):
            routed = jnp.any(routing == expert_index, axis=-1)
            slot_index = (jnp.cumsum(routed.astype(jnp.int32), axis=1) - 1).astype(jnp.int32)
            live_count = jnp.sum(routed.astype(jnp.int32), axis=1)
            live_slot = lax.broadcasted_iota(jnp.int32, (2, capacity), 1) < live_count[:, None]
            inputs = x_blocks[section_index, :, expert_index]
            grads = jnp.where(live_slot[..., None], d_hidden[section_index, :, expert_index], jnp.zeros((), jnp.bfloat16))
            matrix = weights[section_index, expert_index]
            flat_in = inputs.reshape(2 * capacity, width)
            flat_grad = grads.reshape(2 * capacity, hidden_width)
            grad_pre = expert_backward(flat_in, flat_grad, matrix)
            grad_rows = lax.dot_general(grad_pre, matrix, (((1,), (1,)), ((), ())), preferred_element_type=jnp.float32)
            offsets = (jnp.arange(2, dtype=jnp.int32) * capacity)[:, None]
            row_index = (jnp.clip(slot_index, 0, capacity - 1) + offsets).astype(jnp.int32)
            partial_value = jnp.where(routed[..., None], jnp.take(grad_rows, row_index, axis=0), jnp.float32(0.0))
            local_grad = lax.dot_general(flat_in, grad_pre, (((0,), (0,)), ((), ())), preferred_element_type=jnp.float32).astype(jnp.bfloat16)
            return partial_value, local_grad

        partials, local_grads = lax.map(one_expert, jnp.arange(EXPERTS, dtype=jnp.int32))
        summed = jnp.sum(partials, axis=0).astype(jnp.bfloat16)
        return summed, local_grads

    summed, local_grads = lax.map(one_section, jnp.arange(SECTIONS, dtype=jnp.int32))
    zero_row = jnp.zeros((1,) + summed.shape[2:], jnp.bfloat16)
    from_next = jnp.concatenate([summed[1:, 0], zero_row], axis=0)
    from_prior = jnp.concatenate([zero_row, summed[:-1, 1]], axis=0)
    d_in = jnp.stack([from_next, from_prior], axis=2)
    twin_grad = jnp.roll(local_grads, SECTIONS // 2, axis=0)
    d_weights = (local_grads.astype(jnp.float32) + twin_grad.astype(jnp.float32)).astype(jnp.bfloat16)
    return d_in, d_weights
```

```python
import jax
import jax.numpy as jnp
from jax import lax
from jax.experimental import pallas as pl
from jax.experimental.pallas import tpu as pltpu
from jax.sharding import PartitionSpec as P

MESH = pl.DeviceIdType.MESH
BF16 = jnp.bfloat16
F32 = jnp.float32


def gradients(x, h, w):
    ff = h.shape[1]
    projected = jnp.dot(x, w, preferred_element_type=F32)
    gate = projected[:, :ff]
    up = projected[:, ff:]
    sg = 1.0 / (1.0 + jnp.exp(-gate))
    hf = h.astype(F32)
    hs = hf * sg
    grad_gate = hs * up * (1.0 + gate * (1.0 - sg))
    grad_up = hs * gate
    return grad_gate.astype(BF16), grad_up.astype(BF16)


def exchange_kernel(
    routes, x_hbm, h_hbm, w_hbm,
    d_out, h_twin, local_out,
    x, h, w, g, part, far, near, mid, total, in_sems, sends, recvs,
):
    sections = lax.axis_size("section")
    experts = lax.axis_size("expert")
    s = lax.axis_index("section")
    e = lax.axis_index("expert")
    cap = x.shape[0] // 2
    ff = h.shape[1]
    toks = routes.shape[2]

    def section(step):
        return (lax.rem(s + step + sections, sections), e)

    def expert(step):
        return (s, lax.rem(e + step + experts, experts))

    up, down = expert(1), expert(-1)
    after, before = section(1), section(-1)
    twin = section(sections // 2)

    barrier = pltpu.get_barrier_semaphore()
    for partner in (twin, after, before, up, down):
        pl.semaphore_signal(barrier, inc=1, device_id=partner, device_id_type=MESH)
    loads = [
        pltpu.make_async_copy(src, dst, in_sems.at[i])
        for i, (src, dst) in enumerate(((h_hbm, h), (x_hbm, x), (w_hbm, w)))
    ]
    for load in loads:
        load.start()

    upper = (
        lax.broadcasted_iota(jnp.int32, (toks, toks), 0)
        <= lax.broadcasted_iota(jnp.int32, (toks, toks), 1)
    ).astype(F32).astype(BF16)
    slots = lax.broadcasted_iota(jnp.int32, (cap, toks), 0).astype(F32)
    one_hots, counts = [], []
    for r in range(2):
        named = routes[r]
        routed = (named[0:1] == e) | (named[1:2] == e)
        flags = jnp.where(routed, 1.0, 0.0).astype(F32)
        running = jnp.dot(
            jnp.broadcast_to(flags, (16, toks)).astype(BF16), upper, preferred_element_type=F32
        )[0:1]
        slot = jnp.where(routed, running - 1.0, -1.0)
        one_hots.append(jnp.where(slots == slot, 1.0, 0.0).astype(BF16))
        counts.append(jnp.sum(flags, axis=1, keepdims=True))

    loads[0].wait()
    live_rows = lax.broadcasted_iota(jnp.int32, (cap, ff), 0).astype(F32)
    for r in range(2):
        rows = pl.ds(r * cap, cap)
        h[rows] = jnp.where(live_rows < counts[r], h[rows], jnp.zeros((), BF16))

    loads[1].wait()
    loads[2].wait()
    for r in range(2):
        rows = pl.ds(r * cap, cap)
        grad_gate, grad_up = gradients(x[rows], h[rows], w[...])
        g[rows, :ff] = grad_gate
        g[rows, ff:] = grad_up
        ordered = lax.dot_general(
            one_hots[r], g[rows], (((0,), (0,)), ((), ())), preferred_element_type=F32
        ).astype(BF16)
        grad_rows = lax.dot_general(
            ordered, w[...], (((1,), (1,)), ((), ())), preferred_element_type=F32
        ).astype(BF16)
        part[r] = grad_rows.reshape(part.shape[1:])

    def send(i, src, dst, device):
        copy = pltpu.make_async_remote_copy(
            src_ref=src, dst_ref=dst, send_sem=sends.at[i], recv_sem=recvs.at[i],
            device_id=device, device_id_type=MESH,
        )
        copy.start()
        return copy

    pl.semaphore_wait(barrier, 5)
    far_owner = lax.rem(e + 2, experts)
    up_owner, down_owner = up[1], down[1]
    far_up = send(0, part.at[0, far_owner], far.at[0], up)
    far_down = send(1, part.at[1, far_owner], far.at[1], down)
    near_up = send(2, part.at[1, up_owner], near.at[1], up)
    near_down = send(3, part.at[0, down_owner], near.at[0], down)
    hidden = send(4, h, h_twin, twin)

    far_up.wait_recv()
    mid[0] = (part[0, up_owner].astype(F32) + far[0].astype(F32)).astype(BF16)
    far_down.wait_recv()
    mid[1] = (part[1, down_owner].astype(F32) + far[1].astype(F32)).astype(BF16)
    mid_up = send(5, mid.at[0], total.at[0], up)
    mid_down = send(6, mid.at[1], total.at[1], down)

    local_out[...] = lax.dot_general(
        x[...], g[...], (((0,), (0,)), ((), ())), preferred_element_type=F32
    ).astype(BF16)

    near_up.wait_recv()
    near_down.wait_recv()
    mid_up.wait_recv()
    mid_down.wait_recv()
    far_up.wait_send()
    far_down.wait_send()
    for r in range(2):
        far[r] = (
            part[r, e].astype(F32) + near[r].astype(F32) + total[r].astype(F32)
        ).astype(BF16)
    to_before = send(7, far.at[0], d_out.at[0], before)
    to_after = send(8, far.at[1], d_out.at[1], after)
    for copy in (near_up, near_down, mid_up, mid_down):
        copy.wait_send()
    hidden.wait()
    to_before.wait()
    to_after.wait()


def exchange(routes, x, h, w, toks_owned):
    width = x.shape[1]
    hbm = pl.BlockSpec(memory_space=pl.ANY)
    vmem = pl.BlockSpec(memory_space=pltpu.VMEM)
    block = (2, toks_owned, width)
    return pl.pallas_call(
        exchange_kernel,
        name="exchange",
        out_shape=(
            jax.ShapeDtypeStruct(block, BF16),
            jax.ShapeDtypeStruct(h.shape, BF16),
            jax.ShapeDtypeStruct(w.shape, BF16),
        ),
        in_specs=[vmem, hbm, hbm, hbm],
        out_specs=(hbm, hbm, vmem),
        scratch_shapes=[
            pltpu.VMEM(x.shape, BF16),
            pltpu.VMEM(h.shape, BF16),
            pltpu.VMEM(w.shape, BF16),
            pltpu.VMEM((x.shape[0], w.shape[1]), BF16),
            pltpu.VMEM((2, routes.shape[2] // toks_owned, toks_owned, width), BF16),
            pltpu.VMEM(block, BF16),
            pltpu.VMEM(block, BF16),
            pltpu.VMEM(block, BF16),
            pltpu.VMEM(block, BF16),
            pltpu.SemaphoreType.DMA((3,)),
            pltpu.SemaphoreType.DMA((9,)),
            pltpu.SemaphoreType.DMA((9,)),
        ],
        compiler_params=pltpu.CompilerParams(collective_id=0, has_side_effects=True),
        cost_estimate=pl.CostEstimate(
            flops=2_000_000_000, bytes_accessed=8_000_000, transcendentals=150_000
        ),
    )(routes, x, h, w)


def twin_kernel(x, h, w, local, out, g):
    tile = out.shape[0]
    step = pl.program_id(0)

    @pl.when(step == 0)
    def _():
        ff = h.shape[1]
        grad_gate, grad_up = gradients(x[...], h[...], w[...])
        g[:, :ff] = grad_gate
        g[:, ff:] = grad_up

    columns = pl.ds(pl.multiple_of(step * tile, tile), tile)
    product = lax.dot_general(
        x[:, columns], g[...], (((0,), (0,)), ((), ())), preferred_element_type=F32
    )
    out[...] = (local[...].astype(F32) + product).astype(BF16)


def weight_sum(x, h, w, local):
    tile = 256
    whole = lambda a: pl.BlockSpec(a.shape, lambda i: (0, 0), pipeline_mode=pl.Buffered(1))
    rows = pl.BlockSpec((tile, w.shape[1]), lambda i: (i, 0))
    resident = pl.BlockSpec(memory_space=pltpu.VMEM)
    return pl.pallas_call(
        twin_kernel,
        name="twin_product",
        grid=(w.shape[0] // tile,),
        out_shape=jax.ShapeDtypeStruct(w.shape, BF16),
        in_specs=[resident, whole(h), whole(w), rows],
        out_specs=rows,
        scratch_shapes=[pltpu.VMEM((x.shape[0], w.shape[1]), BF16)],
        cost_estimate=pl.CostEstimate(
            flops=1_200_000_000, bytes_accessed=5_700_000, transcendentals=150_000
        ),
    )(x, h, w, local)


def body(routes, x_blocks, d_hidden, weights):
    sections = lax.axis_size("section")
    experts = lax.axis_size("expert")
    s = lax.axis_index("section")
    named = jnp.transpose(routes[0], (0, 2, 1))
    x = x_blocks.reshape(-1, x_blocks.shape[4])
    h = d_hidden.reshape(-1, d_hidden.shape[4])
    w = weights[0, 0]
    half = sections // 2
    x_twin = lax.ppermute(x, "section", [((i + half) % sections, i) for i in range(sections)])
    pair, h_twin, local = exchange(named, x, h, w, named.shape[2] // experts)
    zero = jnp.zeros((), BF16)
    d_in = jnp.stack(
        [jnp.where(s == sections - 1, zero, pair[0]), jnp.where(s == 0, zero, pair[1])], axis=1
    )
    d_weights = weight_sum(x_twin, h_twin, w, local)
    return (d_in[None], d_weights[None, None])


def solution(mesh):
    in_specs = (
        P("section", None, None, None),
        P("section", None, "expert", None, None),
        P("section", None, "expert", None, None),
        P("section", "expert", None, None),
    )
    out_specs = (P("section", "expert", None, None), P("section", "expert", None, None))
    return jax.shard_map(body, mesh=mesh, in_specs=in_specs, out_specs=out_specs, check_vma=False)
```

```python
import jax
import jax.numpy as jnp
from jax import lax
from jax.experimental import pallas as pl
from jax.experimental.pallas import tpu as pltpu
from jax.sharding import PartitionSpec as P

MESH = pl.DeviceIdType.MESH
BF16 = jnp.bfloat16
F32 = jnp.float32


def gradients(x, h, w):
    ff = h.shape[1]
    projected = jnp.dot(x, w, preferred_element_type=F32)
    gate = projected[:, :ff]
    up = projected[:, ff:]
    sg = 1.0 / (1.0 + jnp.exp(-gate))
    hf = h.astype(F32)
    hs = hf * sg
    grad_gate = hs * up * (1.0 + gate * (1.0 - sg))
    grad_up = hs * gate
    return grad_gate.astype(BF16), grad_up.astype(BF16)


def exchange_kernel(
    routes, x_hbm, h_hbm, w_hbm,
    d_out, most_out, x_last, h_last, w,
    x, h, g, part, far, near, mid, total, x_twin, h_twin, g_twin, acc,
    named_rows, in_sems, sends, recvs, ready,
):
    sections = lax.axis_size("section")
    experts = lax.axis_size("expert")
    s = lax.axis_index("section")
    e = lax.axis_index("expert")
    cap = x.shape[0] // 2
    ff = h.shape[1]
    toks = named_rows.shape[2]
    half = sections // 2
    core = lax.rem(s, 2)

    def section(step):
        return (lax.rem(s + step + sections, sections), e)

    def expert(step):
        return (s, lax.rem(e + step + experts, experts))

    up, down = expert(1), expert(-1)
    after, before = section(1), section(-1)
    twin = section(half)
    mate = (s + 1 - 2 * core, e)

    barrier = pltpu.get_barrier_semaphore()

    def greet(device):
        pl.semaphore_signal(barrier, inc=1, device_id=device, device_id_type=MESH)

    even = s - core
    greet((lax.rem(even + half, sections), e))

    @pl.when(core == 1)
    def _():
        greet(mate)

    odd = even + 1
    greet((odd, up[1]))
    greet((odd, down[1]))
    greet((lax.rem(odd + 2 - 4 * (1 - core) + sections, sections), e))

    loads = [
        pltpu.make_async_copy(src, dst, in_sems.at[i])
        for i, (src, dst) in enumerate(((routes, named_rows), (h_hbm, h), (x_hbm, x), (w_hbm, w)))
    ]
    for load in loads:
        load.start()

    loads[0].wait()
    upper = (
        lax.broadcasted_iota(jnp.int32, (toks, toks), 0)
        <= lax.broadcasted_iota(jnp.int32, (toks, toks), 1)
    ).astype(F32).astype(BF16)
    slots = lax.broadcasted_iota(jnp.int32, (cap, toks), 0).astype(F32)
    one_hots, counts = [], []
    for r in range(2):
        named = named_rows[r]
        routed = (named[0:1] == e) | (named[1:2] == e)
        flags = jnp.where(routed, 1.0, 0.0).astype(F32)
        running = jnp.dot(
            jnp.broadcast_to(flags, (16, toks)).astype(BF16), upper, preferred_element_type=F32
        )[0:1]
        slot = jnp.where(routed, running - 1.0, -1.0)
        one_hots.append(jnp.where(slots == slot, 1.0, 0.0).astype(BF16))
        counts.append(jnp.sum(flags, axis=1, keepdims=True))

    loads[1].wait()
    live_rows = lax.broadcasted_iota(jnp.int32, (cap, ff), 0).astype(F32)
    for r in range(2):
        rows = pl.ds(r * cap, cap)
        h[rows] = jnp.where(live_rows < counts[r], h[rows], jnp.zeros((), BF16))

    @pl.when(core == 0)
    def _():
        pl.semaphore_wait(barrier, 3)
        pl.semaphore_signal(ready, inc=1, device_id=mate, device_id_type=MESH)

    @pl.when(core == 1)
    def _():
        pl.semaphore_wait(ready, 1)

    def send(i, src, dst, device):
        copy = pltpu.make_async_remote_copy(
            src_ref=src, dst_ref=dst, send_sem=sends.at[i], recv_sem=recvs.at[i],
            device_id=device, device_id_type=MESH,
        )
        copy.start()
        return copy

    kept = x_twin.shape[0]
    first = cap
    to_twin = [
        send(8, h.at[pl.ds(0, kept)], h_twin, twin),
        send(9, x_hbm.at[pl.ds(0, first)], x_twin.at[pl.ds(0, first)], twin),
        send(10, x_hbm.at[pl.ds(first, kept - first)], x_twin.at[pl.ds(first, kept - first)], twin),
        send(11, h.at[pl.ds(kept, x_last.shape[0])], h_last, twin),
        send(12, x_hbm.at[pl.ds(kept, x_last.shape[0])], x_last, twin),
    ]

    loads[2].wait()
    loads[3].wait()
    for r in range(2):
        rows = pl.ds(r * cap, cap)
        grad_gate, grad_up = gradients(x[rows], h[rows], w[...])
        g[rows, :ff] = grad_gate
        g[rows, ff:] = grad_up
        ordered = lax.dot_general(
            one_hots[r], g[rows], (((0,), (0,)), ((), ())), preferred_element_type=F32
        ).astype(BF16)
        grad_rows = lax.dot_general(
            ordered, w[...], (((1,), (1,)), ((), ())), preferred_element_type=F32
        ).astype(BF16)
        part[r] = grad_rows.reshape(part.shape[1:])

    @pl.when(core == 1)
    def _():
        pl.semaphore_wait(barrier, 6)
        pl.semaphore_signal(ready, inc=1, device_id=mate, device_id_type=MESH)

    @pl.when(core == 0)
    def _():
        pl.semaphore_wait(ready, 1)

    far_owner = lax.rem(e + 2, experts)
    up_owner, down_owner = up[1], down[1]
    far_up = send(0, part.at[0, far_owner], far.at[0], up)
    far_down = send(1, part.at[1, far_owner], far.at[1], down)
    near_up = send(2, part.at[1, up_owner], near.at[1], up)
    near_down = send(3, part.at[0, down_owner], near.at[0], down)

    acc[...] = lax.dot_general(
        x[...], g[...], (((0,), (0,)), ((), ())), preferred_element_type=F32
    )

    far_up.wait_recv()
    mid[0] = (part[0, up_owner].astype(F32) + far[0].astype(F32)).astype(BF16)
    mid_up = send(4, mid.at[0], total.at[0], up)
    far_down.wait_recv()
    mid[1] = (part[1, down_owner].astype(F32) + far[1].astype(F32)).astype(BF16)
    mid_down = send(5, mid.at[1], total.at[1], down)

    def twin_chunk(start, count):
        rows = pl.ds(start, count)
        grad_gate, grad_up = gradients(x_twin[rows], h_twin[rows], w[...])
        g_twin[rows, :ff] = grad_gate
        g_twin[rows, ff:] = grad_up
        return lax.dot_general(
            x_twin[rows], g_twin[rows], (((0,), (0,)), ((), ())), preferred_element_type=F32
        )

    to_twin[0].wait_recv()
    to_twin[1].wait_recv()
    acc[...] += twin_chunk(0, first)

    near_up.wait_recv()
    near_down.wait_recv()
    mid_up.wait_recv()
    mid_down.wait_recv()
    far_up.wait_send()
    far_down.wait_send()
    for r in range(2):
        far[r] = (
            part[r, e].astype(F32) + near[r].astype(F32) + total[r].astype(F32)
        ).astype(BF16)
    to_before = send(6, far.at[0], d_out.at[0], before)
    to_after = send(7, far.at[1], d_out.at[1], after)

    to_twin[2].wait_recv()
    most_out[...] = (acc[...] + twin_chunk(first, kept - first)).astype(BF16)

    for copy in (near_up, near_down, mid_up, mid_down):
        copy.wait_send()
    to_before.wait()
    to_after.wait()
    for copy in to_twin:
        copy.wait_send()
    to_twin[3].wait_recv()
    to_twin[4].wait_recv()


def exchange(routes, x, h, w, toks_owned, kept):
    width = x.shape[1]
    hbm = pl.BlockSpec(memory_space=pltpu.HBM)
    anywhere = pl.BlockSpec(memory_space=pl.ANY)
    vmem = pl.BlockSpec(memory_space=pltpu.VMEM)
    block = (2, toks_owned, width)
    left = x.shape[0] - kept
    return pl.pallas_call(
        exchange_kernel,
        name="exchange",
        out_shape=(
            jax.ShapeDtypeStruct(block, BF16),
            jax.ShapeDtypeStruct(w.shape, BF16),
            jax.ShapeDtypeStruct((left, width), BF16),
            jax.ShapeDtypeStruct((left, h.shape[1]), BF16),
            jax.ShapeDtypeStruct(w.shape, BF16),
        ),
        in_specs=[hbm, hbm, hbm, hbm],
        out_specs=(anywhere, vmem, anywhere, anywhere, vmem),
        scratch_shapes=[
            pltpu.VMEM(x.shape, BF16),
            pltpu.VMEM(h.shape, BF16),
            pltpu.VMEM((x.shape[0], w.shape[1]), BF16),
            pltpu.VMEM((2, routes.shape[2] // toks_owned, toks_owned, width), BF16),
            pltpu.VMEM(block, BF16),
            pltpu.VMEM(block, BF16),
            pltpu.VMEM(block, BF16),
            pltpu.VMEM(block, BF16),
            pltpu.VMEM((kept, width), BF16),
            pltpu.VMEM((kept, h.shape[1]), BF16),
            pltpu.VMEM((kept, w.shape[1]), BF16),
            pltpu.VMEM(w.shape, F32),
            pltpu.VMEM(routes.shape, jnp.int32),
            pltpu.SemaphoreType.DMA((4,)),
            pltpu.SemaphoreType.DMA((13,)),
            pltpu.SemaphoreType.DMA((13,)),
            pltpu.SemaphoreType.REGULAR,
        ],
        compiler_params=pltpu.CompilerParams(
            collective_id=0, has_side_effects=True, vmem_limit_bytes=40 * 2**20
        ),
        cost_estimate=pl.CostEstimate(
            flops=3_000_000_000, bytes_accessed=8_000_000, transcendentals=300_000
        ),
    )(*(pltpu.with_memory_space_constraint(a, pltpu.HBM) for a in (routes, x, h, w)))


def twin_kernel(x, h, w, local, out, g):
    tile = out.shape[0]
    step = pl.program_id(0)

    @pl.when(step == 0)
    def _():
        ff = h.shape[1]
        grad_gate, grad_up = gradients(x[...], h[...], w[...])
        g[:, :ff] = grad_gate
        g[:, ff:] = grad_up

    columns = pl.ds(pl.multiple_of(step * tile, tile), tile)
    product = lax.dot_general(
        x[:, columns], g[...], (((0,), (0,)), ((), ())), preferred_element_type=F32
    )
    out[...] = (local[...].astype(F32) + product).astype(BF16)


def weight_sum(x, h, w, earlier):
    tile = 256
    whole = pl.BlockSpec(memory_space=pltpu.VMEM)
    rows = pl.BlockSpec((tile, w.shape[1]), lambda i: (i, 0))
    count = x.shape[0]
    return pl.pallas_call(
        twin_kernel,
        name="twin_product",
        grid=(w.shape[0] // tile,),
        out_shape=jax.ShapeDtypeStruct(w.shape, BF16),
        in_specs=[whole, whole, whole, rows],
        out_specs=rows,
        scratch_shapes=[pltpu.VMEM((count, w.shape[1]), BF16)],
        compiler_params=pltpu.CompilerParams(vmem_limit_bytes=16 * 2**20),
        cost_estimate=pl.CostEstimate(
            flops=4 * count * w.size, bytes_accessed=5_000_000, transcendentals=count * h.shape[1]
        ),
    )(x, h, w, earlier)


def body(routes, x_blocks, d_hidden, weights):
    sections = lax.axis_size("section")
    experts = lax.axis_size("expert")
    s = lax.axis_index("section")
    named = jnp.transpose(routes[0], (0, 2, 1))
    x = x_blocks.reshape(-1, x_blocks.shape[4])
    h = d_hidden.reshape(-1, d_hidden.shape[4])
    w = weights[0, 0]
    kept = x.shape[0] * 3 // 4
    pair, most, x_last, h_last, w_held = exchange(named, x, h, w, named.shape[2] // experts, kept)
    zero = jnp.zeros((), BF16)
    d_in = jnp.stack(
        [jnp.where(s == sections - 1, zero, pair[0]), jnp.where(s == 0, zero, pair[1])], axis=1
    )
    d_weights = weight_sum(x_last, h_last, w_held, most)
    return (d_in[None], d_weights[None, None])


def solution(mesh):
    in_specs = (
        P("section", None, None, None),
        P("section", None, "expert", None, None),
        P("section", None, "expert", None, None),
        P("section", "expert", None, None),
    )
    out_specs = (P("section", "expert", None, None), P("section", "expert", None, None))
    return jax.shard_map(body, mesh=mesh, in_specs=in_specs, out_specs=out_specs, check_vma=False)
```

```python
import jax
import jax.numpy as jnp
from jax import lax
from jax.experimental import pallas as pl
from jax.experimental.pallas import tpu as pltpu
from jax.sharding import PartitionSpec as P

MESH = pl.DeviceIdType.MESH
BF16 = jnp.bfloat16
F32 = jnp.float32


def factors(x, w):
    ff = w.shape[1] // 2
    projected = jnp.dot(x, w, preferred_element_type=F32)
    gate = projected[:, :ff]
    sg = 1.0 / (1.0 + jnp.exp(-gate))
    return projected[:, ff:], sg * (1.0 + gate * (1.0 - sg)), gate * sg


def gradients(h, up, for_gate, for_up):
    hf = h.astype(F32)
    return (hf * up * for_gate).astype(BF16), (hf * for_up).astype(BF16)


def exchange_kernel(
    routes, x_hbm, h_hbm, w_hbm,
    d_out, most_out, x_last, h_last, last_factors,
    x, h, w, g, part, far, near, mid, total, x_twin, h_twin, g_twin, acc,
    named_rows, in_sems, sends, recvs, ready,
):
    sections = lax.axis_size("section")
    experts = lax.axis_size("expert")
    s = lax.axis_index("section")
    e = lax.axis_index("expert")
    cap = x.shape[0] // 2
    ff = h.shape[1]
    toks = named_rows.shape[2]
    half = sections // 2
    core = lax.rem(s, 2)

    def section(step):
        return (lax.rem(s + step + sections, sections), e)

    def expert(step):
        return (s, lax.rem(e + step + experts, experts))

    up, down = expert(1), expert(-1)
    after, before = section(1), section(-1)
    twin = section(half)
    mate = (s + 1 - 2 * core, e)

    def is_collector(section_index):
        return lax.rem(section_index, 2) != section_index // half

    collects = is_collector(s)
    barrier = pltpu.get_barrier_semaphore()

    def greet(device):
        pl.semaphore_signal(barrier, inc=1, device_id=device, device_id_type=MESH)

    def collector_at(device):
        index = device[0]
        other = index + 1 - 2 * lax.rem(index, 2)
        return (jnp.where(is_collector(index), index, other), device[1])

    @pl.when(collects)
    def _():
        greet(twin)

    @pl.when(jnp.logical_not(collects))
    def _():
        greet(mate)

    outer = section(2 * core - 1)
    for neighbour in (up, down, outer):
        greet(collector_at(neighbour))

    loads = [
        pltpu.make_async_copy(src, dst, in_sems.at[i])
        for i, (src, dst) in enumerate(((routes, named_rows), (h_hbm, h), (x_hbm, x), (w_hbm, w)))
    ]
    for load in loads:
        load.start()

    loads[0].wait()
    upper = (
        lax.broadcasted_iota(jnp.int32, (toks, toks), 0)
        <= lax.broadcasted_iota(jnp.int32, (toks, toks), 1)
    ).astype(F32).astype(BF16)
    slots = lax.broadcasted_iota(jnp.int32, (cap, toks), 0).astype(F32)
    one_hots, counts = [], []
    for r in range(2):
        named = named_rows[r]
        routed = (named[0:1] == e) | (named[1:2] == e)
        flags = jnp.where(routed, 1.0, 0.0).astype(F32)
        running = jnp.dot(
            jnp.broadcast_to(flags, (16, toks)).astype(BF16), upper, preferred_element_type=F32
        )[0:1]
        slot = jnp.where(routed, running - 1.0, -1.0)
        one_hots.append(jnp.where(slots == slot, 1.0, 0.0).astype(BF16))
        counts.append(jnp.sum(flags, axis=1, keepdims=True))

    loads[1].wait()
    live_rows = lax.broadcasted_iota(jnp.int32, (cap, ff), 0).astype(F32)
    for r in range(2):
        rows = pl.ds(r * cap, cap)
        h[rows] = jnp.where(live_rows < counts[r], h[rows], jnp.zeros((), BF16))

    @pl.when(jnp.logical_not(collects))
    def _():
        pl.semaphore_wait(barrier, 1)
        pl.semaphore_signal(ready, inc=1, device_id=twin, device_id_type=MESH)

    @pl.when(collects)
    def _():
        pl.semaphore_wait(ready, 1)

    def send(i, src, dst, device):
        copy = pltpu.make_async_remote_copy(
            src_ref=src, dst_ref=dst, send_sem=sends.at[i], recv_sem=recvs.at[i],
            device_id=device, device_id_type=MESH,
        )
        copy.start()
        return copy

    kept = x_twin.shape[0]
    first = cap
    kept, left = x_twin.shape[0], x_last.shape[0]
    first = cap
    head, middle, tail = pl.ds(0, first), pl.ds(first, kept - first), pl.ds(kept, left)
    to_twin = [
        send(8, x_hbm.at[head], x_twin.at[head], twin),
        send(9, h.at[pl.ds(0, kept)], h_twin, twin),
        send(10, x_hbm.at[middle], x_twin.at[middle], twin),
        send(11, x_hbm.at[tail], x_last, twin),
        send(12, h.at[tail], h_last, twin),
    ]

    loads[2].wait()
    loads[3].wait()
    for r in range(2):
        rows = pl.ds(r * cap, cap)
        grad_gate, grad_up = gradients(h[rows], *factors(x[rows], w[...]))
        g[rows, :ff] = grad_gate
        g[rows, ff:] = grad_up
        ordered = lax.dot_general(
            one_hots[r], g[rows], (((0,), (0,)), ((), ())), preferred_element_type=F32
        ).astype(BF16)
        grad_rows = lax.dot_general(
            ordered, w[...], (((1,), (1,)), ((), ())), preferred_element_type=F32
        ).astype(BF16)
        part[r] = grad_rows.reshape(part.shape[1:])

    @pl.when(collects)
    def _():
        pl.semaphore_wait(barrier, 7)
        pl.semaphore_signal(ready, inc=1, device_id=mate, device_id_type=MESH)

    @pl.when(jnp.logical_not(collects))
    def _():
        pl.semaphore_wait(ready, 1)

    far_owner = lax.rem(e + 2, experts)
    up_owner, down_owner = up[1], down[1]
    far_up = send(0, part.at[0, far_owner], far.at[0], up)
    far_down = send(1, part.at[1, far_owner], far.at[1], down)
    near_up = send(2, part.at[1, up_owner], near.at[1], up)
    near_down = send(3, part.at[0, down_owner], near.at[0], down)

    acc[...] = lax.dot_general(
        x[...], g[...], (((0,), (0,)), ((), ())), preferred_element_type=F32
    )

    far_up.wait_recv()
    mid[0] = (part[0, up_owner].astype(F32) + far[0].astype(F32)).astype(BF16)
    mid_up = send(4, mid.at[0], total.at[0], up)
    far_down.wait_recv()
    mid[1] = (part[1, down_owner].astype(F32) + far[1].astype(F32)).astype(BF16)
    mid_down = send(5, mid.at[1], total.at[1], down)

    def twin_chunk(start, count):
        rows = pl.ds(start, count)
        grad_gate, grad_up = gradients(h_twin[rows], *factors(x_twin[rows], w[...]))
        g_twin[rows, :ff] = grad_gate
        g_twin[rows, ff:] = grad_up
        return lax.dot_general(
            x_twin[rows], g_twin[rows], (((0,), (0,)), ((), ())), preferred_element_type=F32
        )

    to_twin[0].wait_recv()
    to_twin[1].wait_recv()
    acc[...] += twin_chunk(0, first)

    near_up.wait_recv()
    near_down.wait_recv()
    mid_up.wait_recv()
    mid_down.wait_recv()
    far_up.wait_send()
    far_down.wait_send()
    for r in range(2):
        summed = part[r, e].astype(F32) + near[r].astype(F32) + total[r].astype(F32)
        edge = s == (0 if r == 0 else sections - 1)
        far[r] = jnp.where(edge, 0.0, summed).astype(BF16)
    to_before = send(6, far.at[0], d_out.at[0], before)
    to_after = send(7, far.at[1], d_out.at[1], after)

    to_twin[2].wait_recv()
    most_out[...] = (acc[...] + twin_chunk(first, kept - first)).astype(BF16)

    to_twin[3].wait_recv()
    for i, factor in enumerate(factors(x_last[...], w[...])):
        last_factors[i] = factor
    for copy in (near_up, near_down, mid_up, mid_down):
        copy.wait_send()
    to_before.wait()
    to_after.wait()
    for copy in to_twin:
        copy.wait_send()
    to_twin[4].wait_recv()


def exchange(routes, x, h, w, toks_owned, kept):
    width = x.shape[1]
    hbm = pl.BlockSpec(memory_space=pltpu.HBM)
    anywhere = pl.BlockSpec(memory_space=pl.ANY)
    vmem = pl.BlockSpec(memory_space=pltpu.VMEM)
    block = (2, toks_owned, width)
    left = x.shape[0] - kept
    return pl.pallas_call(
        exchange_kernel,
        name="exchange",
        out_shape=(
            jax.ShapeDtypeStruct(block, BF16),
            jax.ShapeDtypeStruct(w.shape, BF16),
            jax.ShapeDtypeStruct((left, width), BF16),
            jax.ShapeDtypeStruct((left, h.shape[1]), BF16),
            jax.ShapeDtypeStruct((3, left, h.shape[1]), F32),
        ),
        in_specs=[hbm, hbm, hbm, hbm],
        out_specs=(anywhere, vmem, vmem, anywhere, vmem),
        scratch_shapes=[
            pltpu.VMEM(x.shape, BF16),
            pltpu.VMEM(h.shape, BF16),
            pltpu.VMEM(w.shape, BF16),
            pltpu.VMEM((x.shape[0], w.shape[1]), BF16),
            pltpu.VMEM((2, routes.shape[2] // toks_owned, toks_owned, width), BF16),
            pltpu.VMEM(block, BF16),
            pltpu.VMEM(block, BF16),
            pltpu.VMEM(block, BF16),
            pltpu.VMEM(block, BF16),
            pltpu.VMEM((kept, width), BF16),
            pltpu.VMEM((kept, h.shape[1]), BF16),
            pltpu.VMEM((kept, w.shape[1]), BF16),
            pltpu.VMEM(w.shape, F32),
            pltpu.VMEM(routes.shape, jnp.int32),
            pltpu.SemaphoreType.DMA((4,)),
            pltpu.SemaphoreType.DMA((13,)),
            pltpu.SemaphoreType.DMA((13,)),
            pltpu.SemaphoreType.REGULAR,
        ],
        compiler_params=pltpu.CompilerParams(
            collective_id=0, has_side_effects=True, vmem_limit_bytes=40 * 2**20
        ),
        cost_estimate=pl.CostEstimate(
            flops=3_000_000_000, bytes_accessed=8_000_000, transcendentals=300_000
        ),
    )(*(pltpu.with_memory_space_constraint(a, pltpu.HBM) for a in (routes, x, h, w)))


def last_kernel(x, h, ready_factors, earlier, pair, d_weights, d_in, g):
    tile = d_weights.shape[0]
    step = pl.program_id(0)

    @pl.when(step == 0)
    def _():
        ff = h.shape[1]
        grad_gate, grad_up = gradients(h[...], *(ready_factors[i] for i in range(3)))
        g[:, :ff] = grad_gate
        g[:, ff:] = grad_up

    columns = pl.ds(pl.multiple_of(step * tile, tile), tile)
    product = lax.dot_general(
        x[:, columns], g[...], (((0,), (0,)), ((), ())), preferred_element_type=F32
    )
    d_weights[...] = (earlier[...].astype(F32) + product).astype(BF16)
    for r in range(2):
        d_in[:, r, :] = pair[r]


def finish(x, h, ready_factors, earlier, pair):
    steps = 4
    toks, width = pair.shape[1:]
    whole = pl.BlockSpec(memory_space=pltpu.VMEM)
    rows = pl.BlockSpec((earlier.shape[0] // steps, earlier.shape[1]), lambda i: (i, 0))
    count = x.shape[0]
    return pl.pallas_call(
        last_kernel,
        name="finish",
        grid=(steps,),
        out_shape=(
            jax.ShapeDtypeStruct(earlier.shape, BF16),
            jax.ShapeDtypeStruct((toks, 2, width), BF16),
        ),
        in_specs=[
            whole, whole, whole, rows,
            pl.BlockSpec((2, toks // steps, width), lambda i: (0, i, 0)),
        ],
        out_specs=(rows, pl.BlockSpec((toks // steps, 2, width), lambda i: (i, 0, 0))),
        scratch_shapes=[pltpu.VMEM((count, earlier.shape[1]), BF16)],
        compiler_params=pltpu.CompilerParams(vmem_limit_bytes=16 * 2**20),
        cost_estimate=pl.CostEstimate(
            flops=2 * count * earlier.size, bytes_accessed=4_000_000, transcendentals=0
        ),
    )(x, h, ready_factors, earlier, pair)


def body(routes, x_blocks, d_hidden, weights):
    experts = lax.axis_size("expert")
    named = jnp.transpose(routes[0], (0, 2, 1))
    x = x_blocks.reshape(-1, x_blocks.shape[4])
    h = d_hidden.reshape(-1, d_hidden.shape[4])
    w = weights[0, 0]
    kept = x.shape[0] * 3 // 4
    pair, most, x_last, h_last, ready_factors = exchange(
        named, x, h, w, named.shape[2] // experts, kept
    )
    d_weights, d_in = finish(x_last, h_last, ready_factors, most, pair)
    return (d_in[None], d_weights[None, None])


def solution(mesh):
    in_specs = (
        P("section", None, None, None),
        P("section", None, "expert", None, None),
        P("section", None, "expert", None, None),
        P("section", "expert", None, None),
    )
    out_specs = (P("section", "expert", None, None), P("section", "expert", None, None))
    return jax.shard_map(body, mesh=mesh, in_specs=in_specs, out_specs=out_specs, check_vma=False)
```

```python
import jax
import jax.numpy as jnp
from jax import lax
from jax.experimental import pallas as pl
from jax.experimental.pallas import tpu as pltpu
from jax.sharding import PartitionSpec as P

MESH = pl.DeviceIdType.MESH
BF16 = jnp.bfloat16
F32 = jnp.float32


def factors(x, w):
    ff = w.shape[1] // 2
    projected = jnp.dot(x, w, preferred_element_type=F32)
    gate = projected[:, :ff]
    sg = 1.0 / (1.0 + jnp.exp(-gate))
    return projected[:, ff:], sg * (1.0 + gate * (1.0 - sg)), gate * sg


def gradients(h, up, for_gate, for_up):
    hf = h.astype(F32)
    return (hf * up * for_gate).astype(BF16), (hf * for_up).astype(BF16)


def exchange_kernel(
    routes, x_hbm, h_hbm, w_hbm,
    d_out, most_out, x_turned, h_last, last_factors,
    x, h, w, g, part, far, near, mid, total, x_twin, h_twin, acc,
    named_rows, in_sems, sends, recvs, ready,
):
    sections = lax.axis_size("section")
    experts = lax.axis_size("expert")
    s = lax.axis_index("section")
    e = lax.axis_index("expert")
    cap = x.shape[0] // 2
    ff = h.shape[1]
    toks = named_rows.shape[2]
    half = sections // 2
    core = lax.rem(s, 2)

    def section(step):
        return (lax.rem(s + step + sections, sections), e)

    def expert(step):
        return (s, lax.rem(e + step + experts, experts))

    up, down = expert(1), expert(-1)
    after, before = section(1), section(-1)
    twin = section(half)
    mate = (s + 1 - 2 * core, e)

    def is_collector(section_index):
        return lax.rem(section_index, 2) != section_index // half

    collects = is_collector(s)
    barrier = pltpu.get_barrier_semaphore()

    def greet(device):
        pl.semaphore_signal(barrier, inc=1, device_id=device, device_id_type=MESH)

    def collector_at(device):
        index = device[0]
        other = index + 1 - 2 * lax.rem(index, 2)
        return (jnp.where(is_collector(index), index, other), device[1])

    @pl.when(collects)
    def _():
        greet(twin)

    @pl.when(jnp.logical_not(collects))
    def _():
        greet(mate)

    outer = section(2 * core - 1)
    for neighbour in (up, down, outer):
        greet(collector_at(neighbour))

    loads = [
        pltpu.make_async_copy(src, dst, in_sems.at[i])
        for i, (src, dst) in enumerate(((routes, named_rows), (h_hbm, h), (x_hbm, x), (w_hbm, w)))
    ]
    for load in loads:
        load.start()

    loads[0].wait()
    upper = (
        lax.broadcasted_iota(jnp.int32, (toks, toks), 0)
        <= lax.broadcasted_iota(jnp.int32, (toks, toks), 1)
    ).astype(F32).astype(BF16)
    slots = lax.broadcasted_iota(jnp.int32, (cap, toks), 0).astype(F32)
    one_hots, counts = [], []
    for r in range(2):
        named = named_rows[r]
        routed = (named[0:1] == e) | (named[1:2] == e)
        flags = jnp.where(routed, 1.0, 0.0).astype(F32)
        running = jnp.dot(
            jnp.broadcast_to(flags, (16, toks)).astype(BF16), upper, preferred_element_type=F32
        )[0:1]
        slot = jnp.where(routed, running - 1.0, -1.0)
        one_hots.append(jnp.where(slots == slot, 1.0, 0.0).astype(BF16))
        counts.append(jnp.sum(flags, axis=1, keepdims=True))

    loads[1].wait()
    live_rows = lax.broadcasted_iota(jnp.int32, (cap, ff), 0).astype(F32)
    for r in range(2):
        rows = pl.ds(r * cap, cap)
        h[rows] = jnp.where(live_rows < counts[r], h[rows], jnp.zeros((), BF16))

    @pl.when(jnp.logical_not(collects))
    def _():
        pl.semaphore_wait(barrier, 1)
        pl.semaphore_signal(ready, inc=1, device_id=twin, device_id_type=MESH)

    @pl.when(collects)
    def _():
        pl.semaphore_wait(ready, 1)

    def send(i, src, dst, device):
        copy = pltpu.make_async_remote_copy(
            src_ref=src, dst_ref=dst, send_sem=sends.at[i], recv_sem=recvs.at[i],
            device_id=device, device_id_type=MESH,
        )
        copy.start()
        return copy

    kept = x_twin.shape[0]
    first = cap
    count = x.shape[0] // 3
    kept = h_twin.shape[1]
    chunks = [pl.ds(i * count, count) for i in range(3)]
    to_twin = [send(8, h.at[:, pl.ds(0, kept)], h_twin, twin)]
    for i, rows in enumerate(chunks):
        to_twin.append(send(9 + i, x_hbm.at[rows], x_twin.at[rows], twin))
    to_twin.append(send(12, h.at[:, pl.ds(kept, ff - kept)], h_last, twin))

    loads[2].wait()
    loads[3].wait()
    for r in range(2):
        rows = pl.ds(r * cap, cap)
        grad_gate, grad_up = gradients(h[rows], *factors(x[rows], w[...]))
        g[rows, :ff] = grad_gate
        g[rows, ff:] = grad_up
        ordered = lax.dot_general(
            one_hots[r], g[rows], (((0,), (0,)), ((), ())), preferred_element_type=F32
        ).astype(BF16)
        grad_rows = lax.dot_general(
            ordered, w[...], (((1,), (1,)), ((), ())), preferred_element_type=F32
        ).astype(BF16)
        part[r] = grad_rows.reshape(part.shape[1:])

    @pl.when(collects)
    def _():
        pl.semaphore_wait(barrier, 7)
        pl.semaphore_signal(ready, inc=1, device_id=mate, device_id_type=MESH)

    @pl.when(jnp.logical_not(collects))
    def _():
        pl.semaphore_wait(ready, 1)

    far_owner = lax.rem(e + 2, experts)
    up_owner, down_owner = up[1], down[1]
    far_up = send(0, part.at[0, far_owner], far.at[0], up)
    far_down = send(1, part.at[1, far_owner], far.at[1], down)
    near_up = send(2, part.at[1, up_owner], near.at[1], up)
    near_down = send(3, part.at[0, down_owner], near.at[0], down)

    acc[...] = lax.dot_general(
        x[...], g[...], (((0,), (0,)), ((), ())), preferred_element_type=F32
    )

    far_up.wait_recv()
    mid[0] = (part[0, up_owner].astype(F32) + far[0].astype(F32)).astype(BF16)
    mid_up = send(4, mid.at[0], total.at[0], up)
    far_down.wait_recv()
    mid[1] = (part[1, down_owner].astype(F32) + far[1].astype(F32)).astype(BF16)
    mid_down = send(5, mid.at[1], total.at[1], down)

    def twin_chunk(rows):
        up_pre, for_gate, for_up = factors(x_twin[rows], w[...])
        for i, factor in enumerate((up_pre, for_gate, for_up)):
            last_factors[i, rows] = factor[:, kept:]
        grad_gate, grad_up = gradients(
            h_twin[rows], up_pre[:, :kept], for_gate[:, :kept], for_up[:, :kept]
        )
        turned = jnp.transpose(x_twin[rows])
        x_turned[:, rows] = turned
        acc[:, :kept] += jnp.dot(turned, grad_gate, preferred_element_type=F32)
        acc[:, ff:ff + kept] += jnp.dot(turned, grad_up, preferred_element_type=F32)

    to_twin[0].wait_recv()
    for i in range(2):
        to_twin[1 + i].wait_recv()
        twin_chunk(chunks[i])

    near_up.wait_recv()
    near_down.wait_recv()
    mid_up.wait_recv()
    mid_down.wait_recv()
    far_up.wait_send()
    far_down.wait_send()
    for r in range(2):
        summed = part[r, e].astype(F32) + near[r].astype(F32) + total[r].astype(F32)
        edge = s == (0 if r == 0 else sections - 1)
        far[r] = jnp.where(edge, 0.0, summed).astype(BF16)
    to_before = send(6, far.at[0], d_out.at[0], before)
    to_after = send(7, far.at[1], d_out.at[1], after)

    to_twin[3].wait_recv()
    twin_chunk(chunks[2])
    most_out[...] = acc[...].astype(BF16)

    for copy in (near_up, near_down, mid_up, mid_down):
        copy.wait_send()
    to_before.wait()
    to_after.wait()
    for copy in to_twin:
        copy.wait_send()
    to_twin[4].wait_recv()


def exchange(routes, x, h, w, toks_owned, kept):
    width = x.shape[1]
    hbm = pl.BlockSpec(memory_space=pltpu.HBM)
    anywhere = pl.BlockSpec(memory_space=pl.ANY)
    vmem = pl.BlockSpec(memory_space=pltpu.VMEM)
    block = (2, toks_owned, width)
    left = h.shape[1] - kept
    return pl.pallas_call(
        exchange_kernel,
        name="exchange",
        out_shape=(
            jax.ShapeDtypeStruct(block, BF16),
            jax.ShapeDtypeStruct(w.shape, BF16),
            jax.ShapeDtypeStruct((width, x.shape[0]), BF16),
            jax.ShapeDtypeStruct((x.shape[0], left), BF16),
            jax.ShapeDtypeStruct((3, x.shape[0], left), F32),
        ),
        in_specs=[hbm, hbm, hbm, hbm],
        out_specs=(anywhere, vmem, vmem, anywhere, vmem),
        scratch_shapes=[
            pltpu.VMEM(x.shape, BF16),
            pltpu.VMEM(h.shape, BF16),
            pltpu.VMEM(w.shape, BF16),
            pltpu.VMEM((x.shape[0], w.shape[1]), BF16),
            pltpu.VMEM((2, routes.shape[2] // toks_owned, toks_owned, width), BF16),
            pltpu.VMEM(block, BF16),
            pltpu.VMEM(block, BF16),
            pltpu.VMEM(block, BF16),
            pltpu.VMEM(block, BF16),
            pltpu.VMEM(x.shape, BF16),
            pltpu.VMEM((h.shape[0], kept), BF16),
            pltpu.VMEM(w.shape, F32),
            pltpu.VMEM(routes.shape, jnp.int32),
            pltpu.SemaphoreType.DMA((4,)),
            pltpu.SemaphoreType.DMA((13,)),
            pltpu.SemaphoreType.DMA((13,)),
            pltpu.SemaphoreType.REGULAR,
        ],
        compiler_params=pltpu.CompilerParams(
            collective_id=0, has_side_effects=True, vmem_limit_bytes=40 * 2**20
        ),
        cost_estimate=pl.CostEstimate(
            flops=3_000_000_000, bytes_accessed=8_000_000, transcendentals=300_000
        ),
    )(*(pltpu.with_memory_space_constraint(a, pltpu.HBM) for a in (routes, x, h, w)))


def last_kernel(x_turned, h, ready_factors, earlier, pair, d_weights, d_in, product, woven, sems):
    ff = earlier.shape[1] // 2
    left = h.shape[1]
    kept = ff - left
    steps = 4
    tile = earlier.shape[0] // steps
    copies = []

    def put(src, dst):
        copy = pltpu.make_async_copy(src, dst, sems.at[len(copies)])
        copy.start()
        copies.append(copy)

    for start in (0, ff):
        columns = pl.ds(start, kept)
        put(earlier.at[:, columns], d_weights.at[:, columns])
    g = gradients(h[...], *(ready_factors[i] for i in range(3)))
    for i in range(steps):
        rows = pl.ds(i * tile, tile)
        for side in range(2):
            columns = pl.ds(side * ff + kept, left)
            more = jnp.dot(x_turned[rows], g[side], preferred_element_type=F32)
            product[side, rows] = (earlier[rows, columns].astype(F32) + more).astype(BF16)
            put(product.at[side, rows], d_weights.at[rows, columns])
    for r in range(2):
        woven[:, r, :] = pair[r]
    put(woven, d_in)
    for copy in copies:
        copy.wait()


def finish(x_turned, h, ready_factors, earlier, pair):
    toks, width = pair.shape[1:]
    whole = pl.BlockSpec(memory_space=pltpu.VMEM)
    anywhere = pl.BlockSpec(memory_space=pl.ANY)
    return pl.pallas_call(
        last_kernel,
        name="finish",
        out_shape=(
            jax.ShapeDtypeStruct(earlier.shape, BF16),
            jax.ShapeDtypeStruct((toks, 2, width), BF16),
        ),
        in_specs=[whole] * 5,
        out_specs=(anywhere, anywhere),
        scratch_shapes=[
            pltpu.VMEM((2, earlier.shape[0], h.shape[1]), BF16),
            pltpu.VMEM((toks, 2, width), BF16),
            pltpu.SemaphoreType.DMA((11,)),
        ],
        compiler_params=pltpu.CompilerParams(vmem_limit_bytes=16 * 2**20),
        cost_estimate=pl.CostEstimate(
            flops=600_000_000, bytes_accessed=4_000_000, transcendentals=0
        ),
    )(x_turned, h, ready_factors, earlier, pair)


def body(routes, x_blocks, d_hidden, weights):
    experts = lax.axis_size("expert")
    named = jnp.transpose(routes[0], (0, 2, 1))
    x = x_blocks.reshape(-1, x_blocks.shape[4])
    h = d_hidden.reshape(-1, d_hidden.shape[4])
    w = weights[0, 0]
    kept = h.shape[1] * 2 // 3
    pair, most, x_turned, h_last, ready_factors = exchange(
        named, x, h, w, named.shape[2] // experts, kept
    )
    d_weights, d_in = finish(x_turned, h_last, ready_factors, most, pair)
    return (d_in[None], d_weights[None, None])


def solution(mesh):
    in_specs = (
        P("section", None, None, None),
        P("section", None, "expert", None, None),
        P("section", None, "expert", None, None),
        P("section", "expert", None, None),
    )
    out_specs = (P("section", "expert", None, None), P("section", "expert", None, None))
    return jax.shard_map(body, mesh=mesh, in_specs=in_specs, out_specs=out_specs, check_vma=False)
```

```python
import jax
import jax.numpy as jnp
from jax import lax
from jax.experimental import pallas as pl
from jax.experimental.pallas import tpu as pltpu
from jax.sharding import PartitionSpec as P

MESH = pl.DeviceIdType.MESH
BF16 = jnp.bfloat16
F32 = jnp.float32


def factors(x, w):
    ff = w.shape[1] // 2
    projected = jnp.dot(x, w, preferred_element_type=F32)
    gate = projected[:, :ff]
    sg = 1.0 / (1.0 + jnp.exp(-gate))
    return projected[:, ff:], sg * (1.0 + gate * (1.0 - sg)), gate * sg


def gradients(h, up, for_gate, for_up):
    hf = h.astype(F32)
    return (hf * up * for_gate).astype(BF16), (hf * for_up).astype(BF16)


def exchange_kernel(
    routes, x_hbm, h_hbm, w_hbm,
    d_out, most_out, x_turned, h_last, last_factors,
    x, h, w, g, part, far, near, mid, total, x_twin, h_twin, acc,
    named_rows, in_sems, sends, recvs, ready,
):
    sections = lax.axis_size("section")
    experts = lax.axis_size("expert")
    s = lax.axis_index("section")
    e = lax.axis_index("expert")
    cap = x.shape[0] // 2
    ff = h.shape[1]
    toks = named_rows.shape[2]
    half = sections // 2
    core = lax.rem(s, 2)

    def section(step):
        return (lax.rem(s + step + sections, sections), e)

    def expert(step):
        return (s, lax.rem(e + step + experts, experts))

    up, down = expert(1), expert(-1)
    after, before = section(1), section(-1)
    twin = section(half)
    mate = (s + 1 - 2 * core, e)

    def is_collector(section_index):
        return lax.rem(section_index, 2) != section_index // half

    collects = is_collector(s)
    barrier = pltpu.get_barrier_semaphore()

    def greet(device):
        pl.semaphore_signal(barrier, inc=1, device_id=device, device_id_type=MESH)

    def collector_at(device):
        index = device[0]
        other = index + 1 - 2 * lax.rem(index, 2)
        return (jnp.where(is_collector(index), index, other), device[1])

    @pl.when(collects)
    def _():
        greet(twin)

    @pl.when(jnp.logical_not(collects))
    def _():
        greet(mate)

    outer = section(2 * core - 1)
    for neighbour in (up, down, outer):
        greet(collector_at(neighbour))

    loads = [
        pltpu.make_async_copy(src, dst, in_sems.at[i])
        for i, (src, dst) in enumerate(((routes, named_rows), (h_hbm, h), (x_hbm, x), (w_hbm, w)))
    ]
    for load in loads:
        load.start()

    loads[0].wait()
    upper = (
        lax.broadcasted_iota(jnp.int32, (toks, toks), 0)
        <= lax.broadcasted_iota(jnp.int32, (toks, toks), 1)
    ).astype(F32).astype(BF16)
    slots = lax.broadcasted_iota(jnp.int32, (cap, toks), 0).astype(F32)
    one_hots, counts = [], []
    for r in range(2):
        named = named_rows[r]
        routed = (named[0:1] == e) | (named[1:2] == e)
        flags = jnp.where(routed, 1.0, 0.0).astype(F32)
        running = jnp.dot(
            jnp.broadcast_to(flags, (16, toks)).astype(BF16), upper, preferred_element_type=F32
        )[0:1]
        slot = jnp.where(routed, running - 1.0, -1.0)
        one_hots.append(jnp.where(slots == slot, 1.0, 0.0).astype(BF16))
        counts.append(jnp.sum(flags, axis=1, keepdims=True))

    loads[1].wait()
    live_rows = lax.broadcasted_iota(jnp.int32, (cap, ff), 0).astype(F32)
    for r in range(2):
        rows = pl.ds(r * cap, cap)
        h[rows] = jnp.where(live_rows < counts[r], h[rows], jnp.zeros((), BF16))

    @pl.when(jnp.logical_not(collects))
    def _():
        pl.semaphore_wait(barrier, 1)
        pl.semaphore_signal(ready, inc=1, device_id=twin, device_id_type=MESH)

    @pl.when(collects)
    def _():
        pl.semaphore_wait(ready, 1)

    def send(i, src, dst, device):
        copy = pltpu.make_async_remote_copy(
            src_ref=src, dst_ref=dst, send_sem=sends.at[i], recv_sem=recvs.at[i],
            device_id=device, device_id_type=MESH,
        )
        copy.start()
        return copy

    kept = x_twin.shape[0]
    first = cap
    count = x.shape[0] // 3
    kept = h_twin.shape[1]
    chunks = [pl.ds(i * count, count) for i in range(3)]
    to_twin = [send(8, h.at[:, pl.ds(0, kept)], h_twin, twin)]
    for i, rows in enumerate(chunks):
        to_twin.append(send(9 + i, x_hbm.at[rows], x_twin.at[rows], twin))
    to_twin.append(send(12, h.at[:, pl.ds(kept, ff - kept)], h_last, twin))

    loads[2].wait()
    loads[3].wait()
    for r in range(2):
        rows = pl.ds(r * cap, cap)
        grad_gate, grad_up = gradients(h[rows], *factors(x[rows], w[...]))
        g[rows, :ff] = grad_gate
        g[rows, ff:] = grad_up
        ordered = lax.dot_general(
            one_hots[r], g[rows], (((0,), (0,)), ((), ())), preferred_element_type=F32
        ).astype(BF16)
        grad_rows = lax.dot_general(
            ordered, w[...], (((1,), (1,)), ((), ())), preferred_element_type=F32
        ).astype(BF16)
        part[r] = grad_rows.reshape(part.shape[1:])

    @pl.when(collects)
    def _():
        pl.semaphore_wait(barrier, 7)
        pl.semaphore_signal(ready, inc=1, device_id=mate, device_id_type=MESH)

    @pl.when(jnp.logical_not(collects))
    def _():
        pl.semaphore_wait(ready, 1)

    far_owner = lax.rem(e + 2, experts)
    up_owner, down_owner = up[1], down[1]
    far_up = send(0, part.at[0, far_owner], far.at[0], up)
    far_down = send(1, part.at[1, far_owner], far.at[1], down)
    near_up = send(2, part.at[1, up_owner], near.at[1], up)
    near_down = send(3, part.at[0, down_owner], near.at[0], down)

    acc[...] = lax.dot_general(
        x[...], g[...], (((0,), (0,)), ((), ())), preferred_element_type=F32
    )

    far_up.wait_recv()
    mid[0] = (part[0, up_owner].astype(F32) + far[0].astype(F32)).astype(BF16)
    mid_up = send(4, mid.at[0], total.at[0], up)
    far_down.wait_recv()
    mid[1] = (part[1, down_owner].astype(F32) + far[1].astype(F32)).astype(BF16)
    mid_down = send(5, mid.at[1], total.at[1], down)

    def twin_chunk(rows):
        up_pre, for_gate, for_up = factors(x_twin[rows], w[...])
        for i, factor in enumerate((up_pre, for_gate, for_up)):
            last_factors[i, rows] = factor[:, kept:]
        grad_gate, grad_up = gradients(
            h_twin[rows], up_pre[:, :kept], for_gate[:, :kept], for_up[:, :kept]
        )
        turned = jnp.transpose(x_twin[rows])
        x_turned[:, rows] = turned
        acc[:, :kept] += jnp.dot(turned, grad_gate, preferred_element_type=F32)
        acc[:, ff:ff + kept] += jnp.dot(turned, grad_up, preferred_element_type=F32)

    near_up.wait_recv()
    near_down.wait_recv()
    mid_up.wait_recv()
    mid_down.wait_recv()
    far_up.wait_send()
    far_down.wait_send()
    for r in range(2):
        summed = part[r, e].astype(F32) + near[r].astype(F32) + total[r].astype(F32)
        edge = s == (0 if r == 0 else sections - 1)
        far[r] = jnp.where(edge, 0.0, summed).astype(BF16)
    to_before = send(6, far.at[0], d_out.at[0], before)
    to_after = send(7, far.at[1], d_out.at[1], after)

    to_twin[0].wait_recv()
    for i in range(0, 3):
        to_twin[1 + i].wait_recv()
        twin_chunk(chunks[i])
    most_out[...] = acc[...].astype(BF16)

    for copy in (near_up, near_down, mid_up, mid_down):
        copy.wait_send()
    to_before.wait()
    to_after.wait()
    for copy in to_twin:
        copy.wait_send()
    to_twin[4].wait_recv()


def exchange(routes, x, h, w, toks_owned, kept):
    width = x.shape[1]
    hbm = pl.BlockSpec(memory_space=pltpu.HBM)
    anywhere = pl.BlockSpec(memory_space=pl.ANY)
    vmem = pl.BlockSpec(memory_space=pltpu.VMEM)
    block = (2, toks_owned, width)
    left = h.shape[1] - kept
    return pl.pallas_call(
        exchange_kernel,
        name="exchange",
        out_shape=(
            jax.ShapeDtypeStruct(block, BF16),
            jax.ShapeDtypeStruct(w.shape, BF16),
            jax.ShapeDtypeStruct((width, x.shape[0]), BF16),
            jax.ShapeDtypeStruct((x.shape[0], left), BF16),
            jax.ShapeDtypeStruct((3, x.shape[0], left), F32),
        ),
        in_specs=[hbm, hbm, hbm, hbm],
        out_specs=(anywhere, vmem, vmem, anywhere, vmem),
        scratch_shapes=[
            pltpu.VMEM(x.shape, BF16),
            pltpu.VMEM(h.shape, BF16),
            pltpu.VMEM(w.shape, BF16),
            pltpu.VMEM((x.shape[0], w.shape[1]), BF16),
            pltpu.VMEM((2, routes.shape[2] // toks_owned, toks_owned, width), BF16),
            pltpu.VMEM(block, BF16),
            pltpu.VMEM(block, BF16),
            pltpu.VMEM(block, BF16),
            pltpu.VMEM(block, BF16),
            pltpu.VMEM(x.shape, BF16),
            pltpu.VMEM((h.shape[0], kept), BF16),
            pltpu.VMEM(w.shape, F32),
            pltpu.VMEM(routes.shape, jnp.int32),
            pltpu.SemaphoreType.DMA((4,)),
            pltpu.SemaphoreType.DMA((13,)),
            pltpu.SemaphoreType.DMA((13,)),
            pltpu.SemaphoreType.REGULAR,
        ],
        compiler_params=pltpu.CompilerParams(
            collective_id=0, has_side_effects=True, vmem_limit_bytes=40 * 2**20
        ),
        cost_estimate=pl.CostEstimate(
            flops=3_000_000_000, bytes_accessed=8_000_000, transcendentals=300_000
        ),
    )(*(pltpu.with_memory_space_constraint(a, pltpu.HBM) for a in (routes, x, h, w)))


def last_kernel(x_turned, h, ready_factors, earlier, pair, d_weights, d_in, product, woven, sems):
    ff = earlier.shape[1] // 2
    left = h.shape[1]
    kept = ff - left
    steps = 4
    tile = earlier.shape[0] // steps
    copies = []

    def put(src, dst):
        copy = pltpu.make_async_copy(src, dst, sems.at[len(copies)])
        copy.start()
        copies.append(copy)

    for start in (0, ff):
        columns = pl.ds(start, kept)
        put(earlier.at[:, columns], d_weights.at[:, columns])
    g = gradients(h[...], *(ready_factors[i] for i in range(3)))
    for i in range(steps):
        rows = pl.ds(i * tile, tile)
        for side in range(2):
            columns = pl.ds(side * ff + kept, left)
            more = jnp.dot(x_turned[rows], g[side], preferred_element_type=F32)
            product[side, rows] = (earlier[rows, columns].astype(F32) + more).astype(BF16)
            put(product.at[side, rows], d_weights.at[rows, columns])
    for r in range(2):
        woven[:, r, :] = pair[r]
    put(woven, d_in)
    for copy in copies:
        copy.wait()


def finish(x_turned, h, ready_factors, earlier, pair):
    toks, width = pair.shape[1:]
    whole = pl.BlockSpec(memory_space=pltpu.VMEM)
    anywhere = pl.BlockSpec(memory_space=pl.ANY)
    return pl.pallas_call(
        last_kernel,
        name="finish",
        out_shape=(
            jax.ShapeDtypeStruct(earlier.shape, BF16),
            jax.ShapeDtypeStruct((toks, 2, width), BF16),
        ),
        in_specs=[whole] * 5,
        out_specs=(anywhere, anywhere),
        scratch_shapes=[
            pltpu.VMEM((2, earlier.shape[0], h.shape[1]), BF16),
            pltpu.VMEM((toks, 2, width), BF16),
            pltpu.SemaphoreType.DMA((11,)),
        ],
        compiler_params=pltpu.CompilerParams(vmem_limit_bytes=16 * 2**20),
        cost_estimate=pl.CostEstimate(
            flops=600_000_000, bytes_accessed=4_000_000, transcendentals=0
        ),
    )(x_turned, h, ready_factors, earlier, pair)


def body(routes, x_blocks, d_hidden, weights):
    experts = lax.axis_size("expert")
    named = jnp.transpose(routes[0], (0, 2, 1))
    x = x_blocks.reshape(-1, x_blocks.shape[4])
    h = d_hidden.reshape(-1, d_hidden.shape[4])
    w = weights[0, 0]
    kept = h.shape[1] * 2 // 3
    pair, most, x_turned, h_last, ready_factors = exchange(
        named, x, h, w, named.shape[2] // experts, kept
    )
    d_weights, d_in = finish(x_turned, h_last, ready_factors, most, pair)
    return (d_in[None], d_weights[None, None])


def solution(mesh):
    in_specs = (
        P("section", None, None, None),
        P("section", None, "expert", None, None),
        P("section", None, "expert", None, None),
        P("section", "expert", None, None),
    )
    out_specs = (P("section", "expert", None, None), P("section", "expert", None, None))
    return jax.shard_map(body, mesh=mesh, in_specs=in_specs, out_specs=out_specs, check_vma=False)
```

```python
import jax
import jax.numpy as jnp
from jax import lax
from jax.experimental import pallas as pl
from jax.experimental.pallas import tpu as pltpu
from jax.sharding import PartitionSpec as P

MESH = pl.DeviceIdType.MESH
BF16 = jnp.bfloat16
F32 = jnp.float32


def factors(x, w):
    ff = w.shape[1] // 2
    projected = jnp.dot(x, w, preferred_element_type=F32)
    gate = projected[:, :ff]
    sg = 1.0 / (1.0 + jnp.exp(-gate))
    return projected[:, ff:], sg * (1.0 + gate * (1.0 - sg)), gate * sg


def gradients(h, up, for_gate, for_up):
    hf = h.astype(F32)
    return (hf * up * for_gate).astype(BF16), (hf * for_up).astype(BF16)


def exchange_kernel(
    routes, x_hbm, h_hbm, w_hbm,
    d_out, most_out, x_turned, h_last, last_factors,
    x, h, w, g, part, far, near, mid, total, x_twin, h_twin, acc,
    named_rows, in_sems, sends, recvs, ready,
):
    sections = lax.axis_size("section")
    experts = lax.axis_size("expert")
    s = lax.axis_index("section")
    e = lax.axis_index("expert")
    cap = x.shape[0] // 2
    ff = h.shape[1]
    toks = named_rows.shape[2]
    half = sections // 2
    core = lax.rem(s, 2)

    def section(step):
        return (lax.rem(s + step + sections, sections), e)

    def expert(step):
        return (s, lax.rem(e + step + experts, experts))

    up, down = expert(1), expert(-1)
    after, before = section(1), section(-1)
    twin = section(half)
    mate = (s + 1 - 2 * core, e)

    def is_collector(section_index):
        return lax.rem(section_index, 2) != section_index // half

    collects = is_collector(s)
    barrier = pltpu.get_barrier_semaphore()

    def greet(device):
        pl.semaphore_signal(barrier, inc=1, device_id=device, device_id_type=MESH)

    def collector_at(device):
        index = device[0]
        other = index + 1 - 2 * lax.rem(index, 2)
        return (jnp.where(is_collector(index), index, other), device[1])

    @pl.when(collects)
    def _():
        greet(twin)

    @pl.when(jnp.logical_not(collects))
    def _():
        greet(mate)

    outer = section(2 * core - 1)
    for neighbour in (up, down, outer):
        greet(collector_at(neighbour))

    loads = [
        pltpu.make_async_copy(src, dst, in_sems.at[i])
        for i, (src, dst) in enumerate(((routes, named_rows), (h_hbm, h), (x_hbm, x), (w_hbm, w)))
    ]
    for load in loads:
        load.start()

    loads[0].wait()
    upper = (
        lax.broadcasted_iota(jnp.int32, (toks, toks), 0)
        <= lax.broadcasted_iota(jnp.int32, (toks, toks), 1)
    ).astype(F32).astype(BF16)
    slots = lax.broadcasted_iota(jnp.int32, (cap, toks), 0).astype(F32)
    one_hots, counts = [], []
    for r in range(2):
        named = named_rows[r]
        routed = (named[0:1] == e) | (named[1:2] == e)
        flags = jnp.where(routed, 1.0, 0.0).astype(F32)
        running = jnp.dot(
            jnp.broadcast_to(flags, (16, toks)).astype(BF16), upper, preferred_element_type=F32
        )[0:1]
        slot = jnp.where(routed, running - 1.0, -1.0)
        one_hots.append(jnp.where(slots == slot, 1.0, 0.0).astype(BF16))
        counts.append(jnp.sum(flags, axis=1, keepdims=True))

    loads[1].wait()
    live_rows = lax.broadcasted_iota(jnp.int32, (cap, ff), 0).astype(F32)
    for r in range(2):
        rows = pl.ds(r * cap, cap)
        h[rows] = jnp.where(live_rows < counts[r], h[rows], jnp.zeros((), BF16))

    @pl.when(jnp.logical_not(collects))
    def _():
        pl.semaphore_wait(barrier, 1)
        pl.semaphore_signal(ready, inc=1, device_id=twin, device_id_type=MESH)

    @pl.when(collects)
    def _():
        pl.semaphore_wait(ready, 1)

    def send(i, src, dst, device):
        copy = pltpu.make_async_remote_copy(
            src_ref=src, dst_ref=dst, send_sem=sends.at[i], recv_sem=recvs.at[i],
            device_id=device, device_id_type=MESH,
        )
        copy.start()
        return copy

    kept = x_twin.shape[0]
    first = cap
    count = x.shape[0] // 3
    kept = h_twin.shape[1]
    chunks = [pl.ds(i * count, count) for i in range(3)]
    to_twin = [send(8, h.at[:, pl.ds(0, kept)], h_twin, twin)]
    for i, rows in enumerate(chunks):
        to_twin.append(send(9 + i, x_hbm.at[rows], x_twin.at[rows], twin))
    to_twin.append(send(12, h.at[:, pl.ds(kept, ff - kept)], h_last, twin))

    loads[2].wait()
    loads[3].wait()
    for r in range(2):
        rows = pl.ds(r * cap, cap)
        grad_gate, grad_up = gradients(h[rows], *factors(x[rows], w[...]))
        g[rows, :ff] = grad_gate
        g[rows, ff:] = grad_up
        ordered = lax.dot_general(
            one_hots[r], g[rows], (((0,), (0,)), ((), ())), preferred_element_type=F32
        ).astype(BF16)
        grad_rows = lax.dot_general(
            ordered, w[...], (((1,), (1,)), ((), ())), preferred_element_type=F32
        ).astype(BF16)
        part[r] = grad_rows.reshape(part.shape[1:])

    @pl.when(collects)
    def _():
        pl.semaphore_wait(barrier, 7)
        pl.semaphore_signal(ready, inc=1, device_id=mate, device_id_type=MESH)

    @pl.when(jnp.logical_not(collects))
    def _():
        pl.semaphore_wait(ready, 1)

    far_owner = lax.rem(e + 2, experts)
    up_owner, down_owner = up[1], down[1]
    far_up = send(0, part.at[0, far_owner], far.at[0], up)
    far_down = send(1, part.at[1, far_owner], far.at[1], down)
    near_up = send(2, part.at[1, up_owner], near.at[1], up)
    near_down = send(3, part.at[0, down_owner], near.at[0], down)

    acc[...] = lax.dot_general(
        x[...], g[...], (((0,), (0,)), ((), ())), preferred_element_type=F32
    )

    block = part.shape[2] // 2
    halves = [pl.ds(i * block, block) for i in range(2)]
    ways = ((far_up, up_owner, up), (far_down, down_owner, down))
    mids = []
    for arrived, owner, device in ways:
        r = len(mids)
        arrived.wait_recv()
        mid[r] = (part[r, owner].astype(F32) + far[r].astype(F32)).astype(BF16)
        mids.append([
            send(13 + 2 * r + i, mid.at[r, rows], total.at[r, rows], device)
            for i, rows in enumerate(halves)
        ])

    def twin_chunk(rows):
        up_pre, for_gate, for_up = factors(x_twin[rows], w[...])
        for i, factor in enumerate((up_pre, for_gate, for_up)):
            last_factors[i, rows] = factor[:, kept:]
        grad_gate, grad_up = gradients(
            h_twin[rows], up_pre[:, :kept], for_gate[:, :kept], for_up[:, :kept]
        )
        turned = jnp.transpose(x_twin[rows])
        x_turned[:, rows] = turned
        acc[:, :kept] += jnp.dot(turned, grad_gate, preferred_element_type=F32)
        acc[:, ff:ff + kept] += jnp.dot(turned, grad_up, preferred_element_type=F32)

    near_up.wait_recv()
    near_down.wait_recv()
    far_up.wait_send()
    far_down.wait_send()
    shifts = []
    for i, rows in enumerate(halves):
        for r, device in enumerate((before, after)):
            mids[r][i].wait_recv()
            summed = (
                part[r, e, rows].astype(F32) + near[r, rows].astype(F32)
                + total[r, rows].astype(F32)
            )
            edge = s == (0 if r == 0 else sections - 1)
            far[r, rows] = jnp.where(edge, 0.0, summed).astype(BF16)
            shifts.append(
                send(4 + 2 * r + i, far.at[r, rows], d_out.at[r, rows], device)
            )

    to_twin[0].wait_recv()
    for i in range(0, 3):
        to_twin[1 + i].wait_recv()
        twin_chunk(chunks[i])
    most_out[...] = acc[...].astype(BF16)

    for copy in (near_up, near_down, *mids[0], *mids[1]):
        copy.wait_send()
    for copy in shifts:
        copy.wait()
    for copy in to_twin:
        copy.wait_send()
    to_twin[4].wait_recv()


def exchange(routes, x, h, w, toks_owned, kept):
    width = x.shape[1]
    hbm = pl.BlockSpec(memory_space=pltpu.HBM)
    anywhere = pl.BlockSpec(memory_space=pl.ANY)
    vmem = pl.BlockSpec(memory_space=pltpu.VMEM)
    block = (2, toks_owned, width)
    left = h.shape[1] - kept
    return pl.pallas_call(
        exchange_kernel,
        name="exchange",
        out_shape=(
            jax.ShapeDtypeStruct(block, BF16),
            jax.ShapeDtypeStruct(w.shape, BF16),
            jax.ShapeDtypeStruct((width, x.shape[0]), BF16),
            jax.ShapeDtypeStruct((x.shape[0], left), BF16),
            jax.ShapeDtypeStruct((3, x.shape[0], left), F32),
        ),
        in_specs=[hbm, hbm, hbm, hbm],
        out_specs=(anywhere, vmem, vmem, anywhere, vmem),
        scratch_shapes=[
            pltpu.VMEM(x.shape, BF16),
            pltpu.VMEM(h.shape, BF16),
            pltpu.VMEM(w.shape, BF16),
            pltpu.VMEM((x.shape[0], w.shape[1]), BF16),
            pltpu.VMEM((2, routes.shape[2] // toks_owned, toks_owned, width), BF16),
            pltpu.VMEM(block, BF16),
            pltpu.VMEM(block, BF16),
            pltpu.VMEM(block, BF16),
            pltpu.VMEM(block, BF16),
            pltpu.VMEM(x.shape, BF16),
            pltpu.VMEM((h.shape[0], kept), BF16),
            pltpu.VMEM(w.shape, F32),
            pltpu.VMEM(routes.shape, jnp.int32),
            pltpu.SemaphoreType.DMA((4,)),
            pltpu.SemaphoreType.DMA((17,)),
            pltpu.SemaphoreType.DMA((17,)),
            pltpu.SemaphoreType.REGULAR,
        ],
        compiler_params=pltpu.CompilerParams(
            collective_id=0, has_side_effects=True, vmem_limit_bytes=40 * 2**20
        ),
        cost_estimate=pl.CostEstimate(
            flops=3_000_000_000, bytes_accessed=8_000_000, transcendentals=300_000
        ),
    )(*(pltpu.with_memory_space_constraint(a, pltpu.HBM) for a in (routes, x, h, w)))


def last_kernel(x_turned, h, ready_factors, earlier, pair, d_weights, d_in, product, woven, sems):
    ff = earlier.shape[1] // 2
    left = h.shape[1]
    kept = ff - left
    steps = 4
    tile = earlier.shape[0] // steps
    copies = []

    def put(src, dst):
        copy = pltpu.make_async_copy(src, dst, sems.at[len(copies)])
        copy.start()
        copies.append(copy)

    for start in (0, ff):
        columns = pl.ds(start, kept)
        put(earlier.at[:, columns], d_weights.at[:, columns])
    g = gradients(h[...], *(ready_factors[i] for i in range(3)))
    for i in range(steps):
        rows = pl.ds(i * tile, tile)
        for side in range(2):
            columns = pl.ds(side * ff + kept, left)
            more = jnp.dot(x_turned[rows], g[side], preferred_element_type=F32)
            product[side, rows] = (earlier[rows, columns].astype(F32) + more).astype(BF16)
            put(product.at[side, rows], d_weights.at[rows, columns])
    for r in range(2):
        woven[:, r, :] = pair[r]
    put(woven, d_in)
    for copy in copies:
        copy.wait()


def finish(x_turned, h, ready_factors, earlier, pair):
    toks, width = pair.shape[1:]
    whole = pl.BlockSpec(memory_space=pltpu.VMEM)
    anywhere = pl.BlockSpec(memory_space=pl.ANY)
    return pl.pallas_call(
        last_kernel,
        name="finish",
        out_shape=(
            jax.ShapeDtypeStruct(earlier.shape, BF16),
            jax.ShapeDtypeStruct((toks, 2, width), BF16),
        ),
        in_specs=[whole] * 5,
        out_specs=(anywhere, anywhere),
        scratch_shapes=[
            pltpu.VMEM((2, earlier.shape[0], h.shape[1]), BF16),
            pltpu.VMEM((toks, 2, width), BF16),
            pltpu.SemaphoreType.DMA((11,)),
        ],
        compiler_params=pltpu.CompilerParams(vmem_limit_bytes=16 * 2**20),
        cost_estimate=pl.CostEstimate(
            flops=600_000_000, bytes_accessed=4_000_000, transcendentals=0
        ),
    )(x_turned, h, ready_factors, earlier, pair)


def body(routes, x_blocks, d_hidden, weights):
    experts = lax.axis_size("expert")
    named = jnp.transpose(routes[0], (0, 2, 1))
    x = x_blocks.reshape(-1, x_blocks.shape[4])
    h = d_hidden.reshape(-1, d_hidden.shape[4])
    w = weights[0, 0]
    kept = h.shape[1] * 2 // 3
    pair, most, x_turned, h_last, ready_factors = exchange(
        named, x, h, w, named.shape[2] // experts, kept
    )
    d_weights, d_in = finish(x_turned, h_last, ready_factors, most, pair)
    return (d_in[None], d_weights[None, None])


def solution(mesh):
    in_specs = (
        P("section", None, None, None),
        P("section", None, "expert", None, None),
        P("section", None, "expert", None, None),
        P("section", "expert", None, None),
    )
    out_specs = (P("section", "expert", None, None), P("section", "expert", None, None))
    return jax.shard_map(body, mesh=mesh, in_specs=in_specs, out_specs=out_specs, check_vma=False)
```
